32 devices in a mesh: rows: 16 (over z, x, core), cols: 2 (over y).
Axes of the slice: x: 2, y: 2, z: 4, core: 2. Of those that a mesh axis runs over, the one named last changes fastest.
Arguments:
- frames_in: bfloat16 [3, 96, 16, 256], P(None, 'rows', 'cols'), may hold values from -6 to 6
- cotangent: bfloat16 [3, 96, 16, 256], P(None, 'rows', 'cols'), may hold values from -6 to 6
- core: float32 [110592], P(('rows', 'cols')), may hold values from -0.3 to 0.3
- moment_one: float32 [110592], P(('rows', 'cols')), may hold values from -0.6 to 0.6
- moment_two: float32 [110592], P(('rows', 'cols')), may hold values from 0.01 to 0.16
- u_in: bfloat16 [256, 64], replicated, may hold values from -0.375 to 0.375
- u_out: bfloat16 [256, 64], replicated, may hold values from -0.375 to 0.375
Outputs:
- frames_grad: bfloat16 [3, 96, 16, 256], P(None, 'rows', 'cols')
- core_next: float32 [110592], P(('rows', 'cols'))
- moment_one_next: float32 [110592], P(('rows', 'cols'))
- moment_two_next: float32 [110592], P(('rows', 'cols'))
- kernel_next: bfloat16 [27, 256, 256], replicated
The draws below stay inside these ranges and needn't reach their ends.
All inputs are finite; a program needn't handle non-finite values.
Results may differ from the reference program's by a relative error of at most 0.014.
Values may be sent and summed in bfloat16 or wider, within the bound.
A program may use at most 64 MiB of HBM per device.

```python
import math
import jax
import jax.numpy as jnp
from jax import lax

C = 256
RANK = 64
TAPS = 27
FRAMES = 3
H = 96
W = 16
CORE = 110592
NCELLS = 4608


def shard_levels(stream_key, dims, pieces, least, top_value):
    level, own = 1.0, jax.random.fold_in(stream_key, 6)
    for dim, shards_of in pieces:
        draws = jnp.exp(jax.random.uniform(jax.random.fold_in(own, dim), (shards_of,), jnp.float32, least / len(pieces), top_value / len(pieces)))
        level = level * jnp.repeat(draws, dims[dim] // shards_of).reshape([-1 if axis == dim else 1 for axis in range(len(dims))])
    return level


def noise(stream_key, dims, width, most, pieces=(), dtype=jnp.bfloat16):
    loudness = shard_levels(stream_key, dims, pieces, -0.22, 0.18) if pieces else 1.0
    drawn = jax.random.normal(stream_key, dims, jnp.float32) * width * loudness
    return jnp.minimum(jnp.maximum(drawn, -most), most).astype(dtype)


def setup_inputs(seed: int = 0) -> dict:
    key_list = jax.random.split(jax.random.key(seed), 8)
    frames_in = noise(key_list[0], (FRAMES, H, W, C), 1.0, 6.0, ((1, 16), (2, 2)))
    cotangent = noise(key_list[1], (FRAMES, H, W, C), 1.0, 6.0, ((1, 16), (2, 2)))
    core = noise(key_list[2], (CORE,), 0.05, 0.3, ((0, 32),), jnp.float32)
    moment_one = noise(key_list[3], (CORE,), 0.1, 0.6, ((0, 32),), jnp.float32)
    moment_two = jnp.clip(jnp.exp(math.log(0.16) - 2.7725887 * jax.random.uniform(key_list[4], (CORE,), jnp.float32) ** shard_levels(key_list[4], (CORE,), ((0, 32),), -0.2, 0.2)), 0.01, 0.16)
    u_in = noise(key_list[5], (C, RANK), C ** -0.5, 0.375)
    u_out = noise(key_list[6], (C, RANK), C ** -0.5, 0.375)
    return {"frames_in": frames_in, "cotangent": cotangent, "core": core, "moment_one": moment_one, "moment_two": moment_two, "u_in": u_in, "u_out": u_out}


beta_one = 0.9
beta_two = 0.999
learn_rate = 0.06
epsilon = 1e-08
fix_one = 1.0 - 0.9 ** 10
fix_two = 1.0 - 0.999 ** 10

def build(flat_core, u_in, u_out):
    cube = flat_core.reshape(TAPS, RANK, RANK).astype(jnp.bfloat16)
    halfway = jnp.einsum('tpq,oq->tpo', cube.astype(jnp.float32), u_out.astype(jnp.float32), precision=lax.Precision.HIGHEST).astype(jnp.bfloat16)
    kernel = jnp.einsum('ip,tpo->tio', u_in.astype(jnp.float32), halfway.astype(jnp.float32), precision=lax.Precision.HIGHEST)
    return kernel.astype(jnp.bfloat16)

def offsets():
    return [(a, b, c) for a in range(3) for b in range(3) for c in range(3)]

def forward_sum(padded, kernel, frames, rows, cols):
    chans = padded.shape[3]
    total = jnp.zeros((frames * rows * cols, kernel.shape[2]), jnp.float32)
    for tap, (a, b, c) in enumerate(offsets()):
        piece = padded[a:a + frames, b:b + rows, c:c + cols, :].reshape(-1, chans)
        total = total + jnp.dot(piece, kernel[tap], preferred_element_type=jnp.float32)
    return total.reshape(frames, rows, cols, -1)

def backward_sum(padded, kernel, frames, rows, cols):
    chans = padded.shape[3]
    total = jnp.zeros((frames * rows * cols, kernel.shape[1]), jnp.float32)
    for tap, (a, b, c) in enumerate(offsets()):
        piece = padded[2 - a:2 - a + frames, 2 - b:2 - b + rows, 2 - c:2 - c + cols, :].reshape(-1, chans)
        total = total + lax.dot_general(piece, kernel[tap], (((1,), (1,)), ((), ())), preferred_element_type=jnp.float32)
    return total.reshape(frames, rows, cols, -1)

def core_terms(padded, slope, u_in, u_out, frames, rows, cols):
    chans = padded.shape[3]
    shape_pad = padded.shape
    in_proj = jnp.dot(padded.reshape(-1, chans), u_in, preferred_element_type=jnp.float32).astype(jnp.bfloat16)
    in_proj = in_proj.reshape(shape_pad[0], shape_pad[1], shape_pad[2], -1)
    out_proj = jnp.dot(slope.reshape(-1, chans), u_out, preferred_element_type=jnp.float32).astype(jnp.bfloat16)
    grads = []
    for tap, (a, b, c) in enumerate(offsets()):
        piece = in_proj[a:a + frames, b:b + rows, c:c + cols, :].reshape(-1, in_proj.shape[3])
        grads.append(lax.dot_general(piece, out_proj, (((0,), (0,)), ((), ())), preferred_element_type=jnp.float32))
    return jnp.stack(grads).reshape(-1)

def reference(frames_in, cotangent, core, moment_one, moment_two, u_in, u_out):
    frames, rows, cols = (frames_in.shape[0], frames_in.shape[1], frames_in.shape[2])
    kernel = build(core, u_in, u_out)
    width_pad = ((1, 1), (1, 1), (1, 1), (0, 0))
    padded = jnp.pad(frames_in, width_pad)
    pre = forward_sum(padded, kernel, frames, rows, cols)
    sig = jax.nn.sigmoid(pre)
    slope = (cotangent.astype(jnp.float32) * sig * (1.0 + pre * (1.0 - sig))).astype(jnp.bfloat16)
    slope_pad = jnp.pad(slope, width_pad)
    frames_grad = backward_sum(slope_pad, kernel, frames, rows, cols).astype(jnp.bfloat16)
    core_grad = core_terms(padded, slope, u_in, u_out, frames, rows, cols) / math.sqrt(NCELLS)
    moment_one_next = beta_one * moment_one + (1.0 - beta_one) * core_grad
    moment_two_next = beta_two * moment_two + (1.0 - beta_two) * core_grad * core_grad
    core_next = core - learn_rate * (moment_one_next / fix_one) / (jnp.sqrt(moment_two_next / fix_two) + epsilon)
    kernel_next = build(core_next, u_in, u_out)
    return (frames_grad, core_next, moment_one_next, moment_two_next, kernel_next)
```

```python
import functools
import math

import jax
import jax.numpy as jnp
from jax import lax
from jax.experimental import pallas as pl
from jax.experimental.pallas import tpu as pltpu
from jax.sharding import PartitionSpec as P

beta_one = 0.9
beta_two = 0.999
learn_rate = 0.06
epsilon = 1e-08
fix_one = 1.0 - 0.9**10
fix_two = 1.0 - 0.999**10


def extended(block, sides, width):
    for axis, dim in sides:
        count = lax.axis_size(axis)
        forward = [(i, i + 1) for i in range(count - 1)]
        backward = [(target, source) for source, target in forward]
        low = lax.ppermute(
            lax.slice_in_dim(block, block.shape[dim] - width, None, axis=dim), axis, forward
        )
        high = lax.ppermute(lax.slice_in_dim(block, 0, width, axis=dim), axis, backward)
        block = jnp.concatenate([low, block, high], axis=dim)
    return block


def build(flat_core, u_in, u_out):
    rank = u_in.shape[1]
    cube = flat_core.reshape(-1, rank).astype(jnp.bfloat16)
    halfway = lax.dot_general(
        cube, u_out, (((1,), (1,)), ((), ())), preferred_element_type=jnp.float32
    ).astype(jnp.bfloat16)
    halfway = halfway.reshape(-1, rank, u_out.shape[0])
    kernel = jnp.einsum("ip,tpo->tio", u_in, halfway, preferred_element_type=jnp.float32)
    return kernel.astype(jnp.bfloat16)


def offsets():
    return [(a, b, c) for a in range(3) for b in range(3) for c in range(3)]


def forward_sum(padded, kernel, frames, rows, cols):
    chans = padded.shape[3]
    total = jnp.zeros((frames * rows * cols, kernel.shape[2]), jnp.float32)
    for tap, (a, b, c) in enumerate(offsets()):
        piece = padded[a : a + frames, b : b + rows, c : c + cols, :].reshape(-1, chans)
        total = total + jnp.dot(piece, kernel[tap], preferred_element_type=jnp.float32)
    return total.reshape(frames, rows, cols, -1)


def backward_sum(padded, kernel, frames, rows, cols):
    chans = padded.shape[3]
    total = jnp.zeros((frames * rows * cols, kernel.shape[1]), jnp.float32)
    for tap, (a, b, c) in enumerate(offsets()):
        piece = padded[
            2 - a : 2 - a + frames, 2 - b : 2 - b + rows, 2 - c : 2 - c + cols, :
        ].reshape(-1, chans)
        total = total + lax.dot_general(
            piece, kernel[tap], (((1,), (1,)), ((), ())), preferred_element_type=jnp.float32
        )
    return total.reshape(frames, rows, cols, -1)


def core_terms(padded, slope, u_in, u_out, frames, rows, cols):
    chans = padded.shape[3]
    shape_pad = padded.shape
    in_proj = jnp.dot(padded.reshape(-1, chans), u_in, preferred_element_type=jnp.float32).astype(
        jnp.bfloat16
    )
    in_proj = in_proj.reshape(shape_pad[0], shape_pad[1], shape_pad[2], -1)
    out_proj = jnp.dot(slope.reshape(-1, chans), u_out, preferred_element_type=jnp.float32).astype(
        jnp.bfloat16
    )
    grads = []
    for tap, (a, b, c) in enumerate(offsets()):
        piece = in_proj[a : a + frames, b : b + rows, c : c + cols, :].reshape(-1, in_proj.shape[3])
        grads.append(
            lax.dot_general(
                piece, out_proj, (((0,), (0,)), ((), ())), preferred_element_type=jnp.float32
            )
        )
    return jnp.stack(grads).reshape(-1)


def time_pad(tile):
    return jnp.pad(tile, ((1, 1), (0, 0), (0, 0), (0, 0)))


def slope_of(cotangent, pre):
    sig = jax.nn.sigmoid(pre)
    return (cotangent.astype(jnp.float32) * sig * (1.0 + pre * (1.0 - sig))).astype(jnp.bfloat16)


def plain_body(frames_in, cotangent, core, moment_one, moment_two, u_in, u_out):
    frames, rows, cols = (frames_in.shape[0], frames_in.shape[1], frames_in.shape[2])
    whole_core = lax.all_gather(core, ("rows", "cols"), axis=0, tiled=True)
    kernel = build(whole_core, u_in, u_out)
    rimmed = extended(frames_in, (("rows", 1), ("cols", 2)), 1)
    padded = time_pad(rimmed)
    pre = forward_sum(padded, kernel, frames, rows, cols)
    slope = slope_of(cotangent, pre)
    slope_rimmed = extended(slope, (("rows", 1), ("cols", 2)), 1)
    slope_pad = time_pad(slope_rimmed)
    frames_grad = backward_sum(slope_pad, kernel, frames, rows, cols).astype(jnp.bfloat16)
    local_grad = core_terms(padded, slope, u_in, u_out, frames, rows, cols)
    partial_grad = lax.psum_scatter(
        local_grad.astype(jnp.bfloat16), "rows", scatter_dimension=0, tiled=True
    ).astype(jnp.float32)
    core_grad = lax.psum_scatter(partial_grad, "cols", scatter_dimension=0, tiled=True)
    cells = frames * rows * lax.axis_size("rows") * cols * lax.axis_size("cols")
    core_grad = core_grad / math.sqrt(cells)
    moment_one_next = beta_one * moment_one + (1.0 - beta_one) * core_grad
    moment_two_next = beta_two * moment_two + (1.0 - beta_two) * core_grad * core_grad
    core_next = core - learn_rate * (moment_one_next / fix_one) / (
        jnp.sqrt(moment_two_next / fix_two) + epsilon
    )
    new_whole = lax.all_gather(core_next, ("rows", "cols"), axis=0, tiled=True)
    kernel_next = build(new_whole, u_in, u_out)
    return (frames_grad, core_next, moment_one_next, moment_two_next, kernel_next)


MESH = pl.DeviceIdType.MESH
vmem_limit = 33554432
NEIGHBOURS = [(dr, dc) for dr in (-1, 0, 1) for dc in (-1, 0, 1) if (dr, dc) != (0, 0)]


def dot(a, b, dims):
    return lax.dot_general(a, b, (dims, ((), ())), preferred_element_type=jnp.float32)


def pair_matrix(rank):
    row = lax.broadcasted_iota(jnp.int32, (rank, rank), 0)
    col = lax.broadcasted_iota(jnp.int32, (rank, rank), 1)
    half = rank // 2
    source = jnp.where(row < half, 2 * row, 2 * (row - half) + 1)
    return jnp.where(col == source, 1.0, 0.0).astype(jnp.bfloat16)


def shifted(wide, c):
    _, frames, rows, cols, rank = wide.shape
    count = frames * rows * cols
    own = wide[1].reshape(count, rank)
    if c == 1:
        return own
    col = lax.broadcasted_iota(jnp.int32, (count, rank), 0) % cols
    if c == 0:
        side = wide[0].reshape(count, rank)
        return jnp.where(
            col == 0, pltpu.roll(side, count - (cols - 1), 0), pltpu.roll(own, 1, 0)
        )
    side = wide[2].reshape(count, rank)
    return jnp.where(
        col == cols - 1, pltpu.roll(side, cols - 1, 0), pltpu.roll(own, count - 1, 0)
    )


def fill_taps(wide, out, flip):
    _, frames, rows, cols, rank = wide.shape
    cells = (frames - 2) * (rows - 2) * cols
    moved = [
        shifted(wide, c).reshape(frames, rows, cols, rank) for c in range(3)
    ]
    for tap, (a, b, c) in enumerate(offsets()):
        if flip:
            a, b, c = 2 - a, 2 - b, 2 - c
        piece = moved[c][a : a + frames - 2, b : b + rows - 2].reshape(cells, rank)
        out[:, rank * tap : rank * (tap + 1)] = piece.astype(jnp.bfloat16)


def seat(owner, n_cols):
    row, col = owner // n_cols, owner % n_cols
    return row % 2, row // 2 * n_cols + col


def cube_rows(parts, grid_shape, flat, cube):
    _, _, rows, lanes = parts.shape
    count = grid_shape[0] * grid_shape[1]
    rank = lanes // 2
    for owner in range(count):
        piece = parts[seat(owner, grid_shape[1])]
        flat[owner * rows : (owner + 1) * rows, :] = piece.astype(jnp.float32)
    half = rank // 2
    taps = count * rows // half
    whole = flat[...].reshape(taps, half, lanes)
    both = jnp.concatenate([whole[:, :, :rank], whole[:, :, rank:]], axis=1)
    cube[...] = both.reshape(taps * rank, rank).astype(jnp.bfloat16)


def flipped(index, mask):
    result, bit = index, 1
    while bit <= mask:
        if mask & bit:
            result = result + bit * (1 - 2 * lax.rem(lax.div(index, bit), 2))
        bit *= 2
    return result


def step_kernel(
    grid_shape, cells_total,
    x_hbm, cot_hbm, core_hbm, one_hbm, two_hbm, uin_hbm, uout_hbm,
    fg_ref, core_out, one_out, two_out, cube_out, pair_ref, uout_ref,
    x_ref, cot_ref, core_ref, one_ref, two_ref, uin_ref,
    wide_in, wide_out, taps_in, taps_out, flat, cube, parts, parts_next,
    mine, theirs, send, recv,
    halo_send, halo_recv, chip_send, chip_recv, sum_recv, side_send, side_recv, load_sem,
):
    n_rows, n_cols = grid_shape
    n = n_rows * n_cols
    chips = n // 2
    my_row, my_col = lax.axis_index("rows"), lax.axis_index("cols")
    core = lax.rem(my_row, 2)
    other = 1 - core
    chip = lax.div(my_row, 2) * n_cols + my_col
    sibling = (my_row + other - core, my_col)
    frames, rows, cols, chans = x_ref.shape
    cells = frames * rows * cols
    rank = uin_ref.shape[0]
    names = ("core", "u_in", "x", "u_out", "cot", "one", "two")
    pairs = (
        (core_hbm, core_ref), (uin_hbm, uin_ref), (x_hbm, x_ref), (uout_hbm, uout_ref),
        (cot_hbm, cot_ref), (one_hbm, one_ref), (two_hbm, two_ref),
    )
    loads = {
        name: pltpu.make_async_copy(source, target, load_sem.at[i])
        for i, (name, (source, target)) in enumerate(zip(names, pairs))
    }
    for load in loads.values():
        load.start()

    def place(mask, on_core):
        peer = flipped(chip, mask)
        return (2 * lax.div(peer, n_cols) + on_core, lax.rem(peer, n_cols))

    wide_in[...] = jnp.zeros_like(wide_in)
    barrier = pltpu.get_barrier_semaphore()
    for mask in range(chips - 1, -1, -1):
        for on_core in (core, other) if mask else (other,):
            pl.semaphore_signal(
                barrier, inc=1, device_id=place(mask, on_core), device_id_type=MESH
            )
    wide_out[...] = jnp.zeros_like(wide_out)

    def remote(source, target, sent, got, where):
        return pltpu.make_async_remote_copy(
            src_ref=source, dst_ref=target, send_sem=sent, recv_sem=got,
            device_id=where, device_id_type=MESH,
        )

    def to_chip(turn, buffer, mask):
        piece = buffer.at[core, chip]
        return remote(piece, piece, chip_send.at[turn], chip_recv.at[mask - 1], place(mask, core))

    def to_far_side(turn, buffer, mask):
        piece = buffer.at[core, chip]
        return remote(piece, piece, side_send.at[turn], side_recv.at[turn], place(mask, other))

    def to_sibling(turn, buffer, mask):
        piece = buffer.at[core, flipped(chip, mask)]
        return remote(piece, piece, side_send.at[turn], side_recv.at[turn], sibling)

    direct = ()

    def gather_start(turn, buffer):
        for mask in range(chips - 1, 0, -1):
            to_chip(turn, buffer, mask).start()
            if mask in direct:
                to_far_side(turn, buffer, mask).start()
        to_sibling(turn, buffer, 0).start()

    def gather_finish(turn, buffer):
        for mask in range(1, chips):
            piece = buffer.at[core, flipped(chip, mask)]
            remote(
                piece, piece, chip_send.at[turn], chip_recv.at[mask - 1], place(mask, core)
            ).wait_recv()
            if mask not in direct:
                to_sibling(turn, buffer, mask).start()
        remote(
            buffer.at[other], buffer.at[other], side_send.at[turn], side_recv.at[turn], sibling
        ).wait_recv()

    def gather_sent(turn, buffer):
        some = buffer.at[0, pl.ds(0, chips - 1)]
        remote(some, some, chip_send.at[turn], chip_recv.at[0], sibling).wait_send()
        remote(
            buffer.at[0], buffer.at[0], side_send.at[turn], side_recv.at[turn], sibling
        ).wait_send()

    loads["core"].wait()
    parts[core, chip] = core_ref[...].astype(jnp.bfloat16)
    pl.semaphore_wait(barrier, n - 1)
    gather_start(0, parts)
    loads["u_in"].wait()
    perm = pair_matrix(rank)
    u_in = dot(perm, uin_ref[...], ((1,), (0,))).astype(jnp.bfloat16)
    pair_ref[...] = dot(uin_ref[...], perm, ((0,), (1,))).astype(jnp.bfloat16)
    loads["x"].wait()
    x = x_ref[...].astype(jnp.float32).reshape(cells, chans).astype(jnp.bfloat16)
    in_proj = dot(x, u_in, ((1,), (1,))).astype(jnp.bfloat16).astype(jnp.float32)
    wide_in[1, 1 : frames + 1, 1 : rows + 1] = in_proj.reshape(frames, rows, cols, rank)

    def halo_copy(wide, turn, slot):
        dr, dc = NEIGHBOURS[slot]
        inner = slice(1, rows + 1)
        source = {-1: slice(1, 2), 0: inner, 1: slice(rows, rows + 1)}[dr]
        edge = {-1: slice(0, 1), 0: slice(0, cols), 1: slice(cols - 1, cols)}[dc]
        target = {-1: slice(rows + 1, rows + 2), 0: inner, 1: slice(0, 1)}[dr]
        side = 0 if dc == 0 else 1 if n_cols == 2 else 1 + (dc + 1) // 2
        return pltpu.make_async_remote_copy(
            src_ref=wide.at[1, 1 : frames + 1, source, edge],
            dst_ref=wide.at[1 - dc, 1 : frames + 1, target, edge],
            send_sem=halo_send.at[turn, dr + 1, side],
            recv_sem=halo_recv.at[turn, dr + 1, side],
            device_id=(my_row + dr, my_col + dc),
            device_id_type=MESH,
        )

    def there(dr, dc):
        row, col = my_row + dr, my_col + dc
        return (row >= 0) & (row < n_rows) & (col >= 0) & (col < n_cols)

    def halo_each(wide, turn, act, sign):
        for slot, (dr, dc) in enumerate(NEIGHBOURS):
            if (dr != 0 and n_rows == 1) or (dc != 0 and n_cols == 1):
                continue

            @pl.when(there(sign * dr, sign * dc))
            def _():
                act(halo_copy(wide, turn, slot))

    halo_each(wide_in, 0, lambda copy: copy.start(), 1)
    halo_each(wide_in, 0, lambda copy: copy.wait_recv(), -1)
    fill_taps(wide_in, taps_in, False)
    gather_finish(0, parts)
    cube_rows(parts, grid_shape, flat, cube)

    mid = dot(taps_in[...], cube[...], ((1,), (0,))).astype(jnp.bfloat16)
    loads["u_out"].wait()
    u_out = uout_ref[...]
    pre = dot(mid, u_out, ((1,), (0,)))
    loads["cot"].wait()
    cot = cot_ref[...].astype(jnp.float32).reshape(cells, chans)
    sig = 1.0 / (1.0 + jnp.exp(-pre))
    slope = (cot * sig * (1.0 + pre * (1.0 - sig))).astype(jnp.bfloat16)
    out_proj = dot(slope, u_out, ((1,), (1,))).astype(jnp.bfloat16)
    wide_out[1, 1 : frames + 1, 1 : rows + 1] = out_proj.astype(jnp.float32).reshape(
        frames, rows, cols, rank
    )
    halo_each(wide_out, 1, lambda copy: copy.start(), 1)

    grad = dot(taps_in[...], out_proj, ((0,), (0,)))
    taps = grad.shape[0] // rank
    half = rank // 2
    grad = grad.reshape(taps, rank, rank)
    grad = jnp.concatenate([grad[:, :half], grad[:, half:]], axis=2)
    flat[...] = grad.reshape(taps * half, 2 * rank)
    part = core_ref.shape[0]
    for owner in range(n):
        on_core, on_chip = seat(owner, n_cols)
        mine[on_core, on_chip] = flat[owner * part : (owner + 1) * part, :].astype(jnp.bfloat16)
    pair_up = remote(mine.at[other], theirs, side_send.at[1], side_recv.at[1], sibling)
    pair_up.start()
    pair_up.wait_recv()
    for k in range(chips):
        send[k] = (mine[core, k].astype(jnp.float32) + theirs[k].astype(jnp.float32)).astype(
            jnp.bfloat16
        )

    def share(mask):
        return remote(
            send.at[flipped(chip, mask)], recv.at[chip], chip_send.at[1], sum_recv.at[0],
            place(mask, core),
        )

    for mask in range(chips - 1, 0, -1):
        share(mask).start()
    recv[chip] = send[chip]

    halo_each(wide_out, 1, lambda copy: copy.wait_recv(), -1)
    fill_taps(wide_out, taps_out, True)
    total = jnp.zeros((cells, rank), jnp.float32)
    for tap in range(taps):
        span = slice(rank * tap, rank * (tap + 1))
        total = total + dot(taps_out[:, span], cube[span, :], ((1,), (1,)))
    back = dot(total.astype(jnp.bfloat16), u_in, ((1,), (0,)))
    fg_ref[...] = back.reshape(frames, rows, cols, chans).astype(jnp.bfloat16)

    halo_each(wide_in, 0, lambda copy: copy.wait_send(), 1)
    halo_each(wide_out, 1, lambda copy: copy.wait_send(), 1)
    gather_sent(0, parts)
    pair_up.wait_send()
    loads["one"].wait()
    loads["two"].wait()
    some = recv.at[pl.ds(0, chips - 1)]
    shares = remote(some, some, chip_send.at[1], sum_recv.at[0], sibling)
    shares.wait_recv()
    summed = recv[0].astype(jnp.float32)
    for k in range(1, chips):
        summed = summed + recv[k].astype(jnp.float32)
    core_grad = summed / math.sqrt(cells_total)
    one_next = beta_one * one_ref[...] + (1.0 - beta_one) * core_grad
    two_next = beta_two * two_ref[...] + (1.0 - beta_two) * core_grad * core_grad
    core_next = core_ref[...] - learn_rate * (one_next / fix_one) / (
        jnp.sqrt(two_next / fix_two) + epsilon
    )
    parts_next[core, chip] = core_next.astype(jnp.bfloat16)
    gather_start(2, parts_next)
    core_out[...] = core_next
    one_out[...] = one_next
    two_out[...] = two_next
    shares.wait_send()
    gather_finish(2, parts_next)
    cube_rows(parts_next, grid_shape, flat, cube_out)
    gather_sent(2, parts_next)


def build_kernel(
    group, cube_ref, uin_ref, uout_ref, fg_from, core_from, one_from, two_from,
    out_hbm, fg_to, core_to, one_to, two_to, out_ref, side_sem, out_sem,
):
    rank = uin_ref.shape[1]
    inner = (fg_from, core_from, one_from, two_from)
    final = (fg_to, core_to, one_to, two_to)
    sides = [
        pltpu.make_async_copy(source, target, side_sem.at[i])
        for i, (source, target) in enumerate(zip(inner, final))
    ]
    u_in = uin_ref[...]
    u_out = uout_ref[...]
    copies = []
    for first in range(0, out_ref.shape[0], group):
        cube = cube_ref[rank * first : rank * (first + group), :]
        halfway = dot(cube, u_out, ((1,), (0,))).astype(jnp.bfloat16)
        for tap in range(group):
            span = slice(rank * tap, rank * (tap + 1))
            out_ref[first + tap] = dot(u_in, halfway[span], ((1,), (0,))).astype(jnp.bfloat16)
        block = pl.ds(first, group)
        copy = pltpu.make_async_copy(
            out_ref.at[block], out_hbm.at[block], out_sem.at[first // group]
        )
        copy.start()
        copies.append(copy)
        if first == 0:
            for side in sides:
                side.start()
    for copy in sides + copies:
        copy.wait()


def fused_body(frames_in, cotangent, core, moment_one, moment_two, u_in, u_out):
    frames, rows, cols, chans = frames_in.shape
    rank = u_in.shape[1]
    grid_shape = (lax.axis_size("rows"), lax.axis_size("cols"))
    n = grid_shape[0] * grid_shape[1]
    chips = n // 2
    lanes = 2 * rank
    part = core.shape[0] // lanes
    taps = n * core.shape[0] // (rank * rank)
    cells = frames * rows * cols
    sides_of = 2 if grid_shape[1] == 2 else 3
    f32, bf16 = jnp.float32, jnp.bfloat16
    hbm = pl.BlockSpec(memory_space=pltpu.HBM)
    vmem = pl.BlockSpec(memory_space=pltpu.VMEM)
    block = pltpu.VMEM(frames_in.shape, bf16)
    flat_vmem = pltpu.VMEM((part, lanes), f32)
    factor = pltpu.VMEM((rank, chans), bf16)
    cube_vmem = pltpu.VMEM((taps * rank, rank), bf16)
    flat_shape = jax.ShapeDtypeStruct((part, lanes), f32)
    wide = pltpu.VMEM((3, frames + 2, rows + 2, cols, rank), f32)
    pieces = pltpu.VMEM((2, chips, part, lanes), bf16)
    sums = pltpu.VMEM((chips, part, lanes), bf16)
    in_hbm = functools.partial(pltpu.with_memory_space_constraint, memory_space=pltpu.HBM)
    in_vmem = functools.partial(pltpu.with_memory_space_constraint, memory_space=pltpu.VMEM)
    *sides, cube_next, uin_next, uout_next = pl.pallas_call(
        functools.partial(step_kernel, grid_shape, cells * n),
        out_shape=(
            block,
            flat_vmem,
            flat_vmem,
            flat_vmem,
            cube_vmem,
            pltpu.VMEM((chans, rank), bf16),
            factor,
        ),
        in_specs=[hbm] * 7,
        out_specs=[vmem] * 7,
        scratch_shapes=[
            block,
            block,
            flat_vmem,
            flat_vmem,
            flat_vmem,
            factor,
            wide,
            wide,
            pltpu.VMEM((cells, taps * rank), bf16),
            pltpu.VMEM((cells, taps * rank), bf16),
            pltpu.VMEM((n * part, lanes), f32),
            pltpu.VMEM((taps * rank, rank), bf16),
            pieces,
            pieces,
            pieces,
            sums,
            sums,
            sums,
            pltpu.SemaphoreType.DMA((2, 3, sides_of)),
            pltpu.SemaphoreType.DMA((2, 3, sides_of)),
            pltpu.SemaphoreType.DMA((3,)),
            pltpu.SemaphoreType.DMA((chips - 1,)),
            pltpu.SemaphoreType.DMA((1,)),
            pltpu.SemaphoreType.DMA((3,)),
            pltpu.SemaphoreType.DMA((3,)),
            pltpu.SemaphoreType.DMA((7,)),
        ],
        compiler_params=pltpu.CompilerParams(
            collective_id=0, has_side_effects=True, vmem_limit_bytes=vmem_limit
        ),
        name="step",
    )(
        in_hbm(frames_in),
        in_hbm(cotangent),
        in_hbm(core.reshape(part, lanes)),
        in_hbm(moment_one.reshape(part, lanes)),
        in_hbm(moment_two.reshape(part, lanes)),
        in_hbm(u_in.T),
        in_hbm(u_out.T),
    )
    group = 9 if taps % 9 == 0 else 1
    kernel_next, fg, core_next, one_next, two_next = pl.pallas_call(
        functools.partial(build_kernel, group),
        out_shape=(
            jax.ShapeDtypeStruct((taps, chans, chans), bf16),
            jax.ShapeDtypeStruct(frames_in.shape, bf16),
            flat_shape,
            flat_shape,
            flat_shape,
        ),
        in_specs=[vmem] * 7,
        out_specs=[hbm] * 5,
        scratch_shapes=[
            pltpu.VMEM((taps, chans, chans), bf16),
            pltpu.SemaphoreType.DMA((4,)),
            pltpu.SemaphoreType.DMA((taps // group,)),
        ],
        compiler_params=pltpu.CompilerParams(vmem_limit_bytes=vmem_limit),
        name="build",
    )(*(in_vmem(array) for array in (cube_next, uin_next, uout_next, *sides)))
    return (
        fg,
        core_next.reshape(-1),
        one_next.reshape(-1),
        two_next.reshape(-1),
        kernel_next,
    )


def body(frames_in, cotangent, core, moment_one, moment_two, u_in, u_out):
    lanes = 2 * u_in.shape[1]
    aligned = lanes == 128 and core.shape[0] % lanes == 0 and frames_in.shape[2] == 8
    chips = lax.axis_size("rows") * lax.axis_size("cols") // 2
    if aligned and lax.axis_size("rows") % 2 == 0 and chips & (chips - 1) == 0:
        step = fused_body
    else:
        step = plain_body
    return step(frames_in, cotangent, core, moment_one, moment_two, u_in, u_out)


def solution(mesh):
    in_specs = (
        P(None, "rows", "cols", None),
        P(None, "rows", "cols", None),
        P(("rows", "cols")),
        P(("rows", "cols")),
        P(("rows", "cols")),
        P(),
        P(),
    )
    out_specs = (
        P(None, "rows", "cols", None),
        P(("rows", "cols")),
        P(("rows", "cols")),
        P(("rows", "cols")),
        P(),
    )
    return jax.shard_map(body, mesh=mesh, in_specs=in_specs, out_specs=out_specs, check_vma=False)
```

```python
import functools
import math

import jax
import jax.numpy as jnp
from jax import lax
from jax.experimental import pallas as pl
from jax.experimental.pallas import tpu as pltpu
from jax.sharding import PartitionSpec as P

beta_one = 0.9
beta_two = 0.999
learn_rate = 0.06
epsilon = 1e-08
fix_one = 1.0 - 0.9**10
fix_two = 1.0 - 0.999**10


def extended(block, sides, width):
    for axis, dim in sides:
        count = lax.axis_size(axis)
        forward = [(i, i + 1) for i in range(count - 1)]
        backward = [(target, source) for source, target in forward]
        low = lax.ppermute(
            lax.slice_in_dim(block, block.shape[dim] - width, None, axis=dim), axis, forward
        )
        high = lax.ppermute(lax.slice_in_dim(block, 0, width, axis=dim), axis, backward)
        block = jnp.concatenate([low, block, high], axis=dim)
    return block


def build(flat_core, u_in, u_out):
    rank = u_in.shape[1]
    cube = flat_core.reshape(-1, rank).astype(jnp.bfloat16)
    halfway = lax.dot_general(
        cube, u_out, (((1,), (1,)), ((), ())), preferred_element_type=jnp.float32
    ).astype(jnp.bfloat16)
    halfway = halfway.reshape(-1, rank, u_out.shape[0])
    kernel = jnp.einsum("ip,tpo->tio", u_in, halfway, preferred_element_type=jnp.float32)
    return kernel.astype(jnp.bfloat16)


def offsets():
    return [(a, b, c) for a in range(3) for b in range(3) for c in range(3)]


def forward_sum(padded, kernel, frames, rows, cols):
    chans = padded.shape[3]
    total = jnp.zeros((frames * rows * cols, kernel.shape[2]), jnp.float32)
    for tap, (a, b, c) in enumerate(offsets()):
        piece = padded[a : a + frames, b : b + rows, c : c + cols, :].reshape(-1, chans)
        total = total + jnp.dot(piece, kernel[tap], preferred_element_type=jnp.float32)
    return total.reshape(frames, rows, cols, -1)


def backward_sum(padded, kernel, frames, rows, cols):
    chans = padded.shape[3]
    total = jnp.zeros((frames * rows * cols, kernel.shape[1]), jnp.float32)
    for tap, (a, b, c) in enumerate(offsets()):
        piece = padded[
            2 - a : 2 - a + frames, 2 - b : 2 - b + rows, 2 - c : 2 - c + cols, :
        ].reshape(-1, chans)
        total = total + lax.dot_general(
            piece, kernel[tap], (((1,), (1,)), ((), ())), preferred_element_type=jnp.float32
        )
    return total.reshape(frames, rows, cols, -1)


def core_terms(padded, slope, u_in, u_out, frames, rows, cols):
    chans = padded.shape[3]
    shape_pad = padded.shape
    in_proj = jnp.dot(padded.reshape(-1, chans), u_in, preferred_element_type=jnp.float32).astype(
        jnp.bfloat16
    )
    in_proj = in_proj.reshape(shape_pad[0], shape_pad[1], shape_pad[2], -1)
    out_proj = jnp.dot(slope.reshape(-1, chans), u_out, preferred_element_type=jnp.float32).astype(
        jnp.bfloat16
    )
    grads = []
    for tap, (a, b, c) in enumerate(offsets()):
        piece = in_proj[a : a + frames, b : b + rows, c : c + cols, :].reshape(-1, in_proj.shape[3])
        grads.append(
            lax.dot_general(
                piece, out_proj, (((0,), (0,)), ((), ())), preferred_element_type=jnp.float32
            )
        )
    return jnp.stack(grads).reshape(-1)


def time_pad(tile):
    return jnp.pad(tile, ((1, 1), (0, 0), (0, 0), (0, 0)))


def slope_of(cotangent, pre):
    sig = jax.nn.sigmoid(pre)
    return (cotangent.astype(jnp.float32) * sig * (1.0 + pre * (1.0 - sig))).astype(jnp.bfloat16)


def plain_body(frames_in, cotangent, core, moment_one, moment_two, u_in, u_out):
    frames, rows, cols = (frames_in.shape[0], frames_in.shape[1], frames_in.shape[2])
    whole_core = lax.all_gather(core, ("rows", "cols"), axis=0, tiled=True)
    kernel = build(whole_core, u_in, u_out)
    rimmed = extended(frames_in, (("rows", 1), ("cols", 2)), 1)
    padded = time_pad(rimmed)
    pre = forward_sum(padded, kernel, frames, rows, cols)
    slope = slope_of(cotangent, pre)
    slope_rimmed = extended(slope, (("rows", 1), ("cols", 2)), 1)
    slope_pad = time_pad(slope_rimmed)
    frames_grad = backward_sum(slope_pad, kernel, frames, rows, cols).astype(jnp.bfloat16)
    local_grad = core_terms(padded, slope, u_in, u_out, frames, rows, cols)
    partial_grad = lax.psum_scatter(
        local_grad.astype(jnp.bfloat16), "rows", scatter_dimension=0, tiled=True
    ).astype(jnp.float32)
    core_grad = lax.psum_scatter(partial_grad, "cols", scatter_dimension=0, tiled=True)
    cells = frames * rows * lax.axis_size("rows") * cols * lax.axis_size("cols")
    core_grad = core_grad / math.sqrt(cells)
    moment_one_next = beta_one * moment_one + (1.0 - beta_one) * core_grad
    moment_two_next = beta_two * moment_two + (1.0 - beta_two) * core_grad * core_grad
    core_next = core - learn_rate * (moment_one_next / fix_one) / (
        jnp.sqrt(moment_two_next / fix_two) + epsilon
    )
    new_whole = lax.all_gather(core_next, ("rows", "cols"), axis=0, tiled=True)
    kernel_next = build(new_whole, u_in, u_out)
    return (frames_grad, core_next, moment_one_next, moment_two_next, kernel_next)


MESH = pl.DeviceIdType.MESH
vmem_limit = 33554432
NEIGHBOURS = [(dr, dc) for dr in (-1, 0, 1) for dc in (-1, 0, 1) if (dr, dc) != (0, 0)]


def dot(a, b, dims):
    return lax.dot_general(a, b, (dims, ((), ())), preferred_element_type=jnp.float32)


def pair_matrix(rank):
    row = lax.broadcasted_iota(jnp.int32, (rank, rank), 0)
    col = lax.broadcasted_iota(jnp.int32, (rank, rank), 1)
    half = rank // 2
    source = jnp.where(row < half, 2 * row, 2 * (row - half) + 1)
    return jnp.where(col == source, 1.0, 0.0).astype(jnp.bfloat16)


def shifted(wide, c):
    _, frames, rows, cols, rank = wide.shape
    count = frames * rows * cols
    own = wide[1].reshape(count, rank)
    if c == 1:
        return own
    col = lax.broadcasted_iota(jnp.int32, (count, rank), 0) % cols
    if c == 0:
        side = wide[0].reshape(count, rank)
        return jnp.where(
            col == 0, pltpu.roll(side, count - (cols - 1), 0), pltpu.roll(own, 1, 0)
        )
    side = wide[2].reshape(count, rank)
    return jnp.where(
        col == cols - 1, pltpu.roll(side, cols - 1, 0), pltpu.roll(own, count - 1, 0)
    )


def fill_taps(wide, out, flip):
    _, frames, rows, cols, rank = wide.shape
    cells = (frames - 2) * (rows - 2) * cols
    moved = [
        shifted(wide, c).reshape(frames, rows, cols, rank) for c in range(3)
    ]
    for tap, (a, b, c) in enumerate(offsets()):
        if flip:
            a, b, c = 2 - a, 2 - b, 2 - c
        piece = moved[c][a : a + frames - 2, b : b + rows - 2].reshape(cells, rank)
        out[:, rank * tap : rank * (tap + 1)] = piece.astype(jnp.bfloat16)


def seat(owner, n_cols):
    row, col = owner // n_cols, owner % n_cols
    return row % 2, row // 2 * n_cols + col


def cube_rows(parts, grid_shape, flat, cube):
    _, _, rows, lanes = parts.shape
    count = grid_shape[0] * grid_shape[1]
    rank = lanes // 2
    for owner in range(count):
        piece = parts[seat(owner, grid_shape[1])]
        flat[owner * rows : (owner + 1) * rows, :] = piece.astype(jnp.float32)
    half = rank // 2
    taps = count * rows // half
    whole = flat[...].reshape(taps, half, lanes)
    both = jnp.concatenate([whole[:, :, :rank], whole[:, :, rank:]], axis=1)
    cube[...] = both.reshape(taps * rank, rank).astype(jnp.bfloat16)


def flipped(index, mask):
    result, bit = index, 1
    while bit <= mask:
        if mask & bit:
            result = result + bit * (1 - 2 * lax.rem(lax.div(index, bit), 2))
        bit *= 2
    return result


def step_kernel(
    grid_shape, cells_total,
    x_hbm, cot_hbm, core_hbm, one_hbm, two_hbm, uin_hbm, uout_hbm,
    fg_ref, core_out, one_out, two_out, cube_out, pair_ref, uout_ref,
    x_ref, cot_ref, core_ref, one_ref, two_ref, uin_ref,
    wide_in, wide_out, taps_in, taps_out, flat, cube, parts, parts_next,
    mine, theirs, send, recv,
    halo_send, halo_recv, chip_send, plane_recv, sum_recv, side_send, side_recv, load_sem,
):
    n_rows, n_cols = grid_shape
    n = n_rows * n_cols
    chips = n // 2
    my_row, my_col = lax.axis_index("rows"), lax.axis_index("cols")
    core = lax.rem(my_row, 2)
    other = 1 - core
    chip = lax.div(my_row, 2) * n_cols + my_col
    sibling = (my_row + other - core, my_col)
    frames, rows, cols, chans = x_ref.shape
    cells = frames * rows * cols
    rank = uin_ref.shape[0]
    names = ("core", "u_in", "x", "u_out", "cot", "one", "two")
    pairs = (
        (core_hbm, core_ref), (uin_hbm, uin_ref), (x_hbm, x_ref), (uout_hbm, uout_ref),
        (cot_hbm, cot_ref), (one_hbm, one_ref), (two_hbm, two_ref),
    )
    loads = {
        name: pltpu.make_async_copy(source, target, load_sem.at[i])
        for i, (name, (source, target)) in enumerate(zip(names, pairs))
    }
    for load in loads.values():
        load.start()

    def seat_of(peer, on_core):
        return (2 * lax.div(peer, n_cols) + on_core, lax.rem(peer, n_cols))

    wide_in[...] = jnp.zeros_like(wide_in)
    near = min(4, chips)
    planes = chips // near
    plane = lax.div(chip, near)
    barrier = pltpu.get_barrier_semaphore()
    for mask in range(chips - 1, -1, -1):
        for on_core in (core, other) if mask else (other,):
            pl.semaphore_signal(
                barrier, inc=1, device_id=seat_of(flipped(chip, mask), on_core),
                device_id_type=MESH,
            )
    wide_out[...] = jnp.zeros_like(wide_out)

    def remote(source, target, sent, got, where):
        return pltpu.make_async_remote_copy(
            src_ref=source, dst_ref=target, send_sem=sent, recv_sem=got,
            device_id=where, device_id_type=MESH,
        )

    def shift_of(peer):
        return lax.rem(plane - lax.div(peer, near) + planes, planes)

    def to_sibling(turn, buffer, step):
        group = buffer.at[core, pl.ds(near * lax.rem(plane + step, planes), near)]
        return remote(group, group, side_send.at[turn], side_recv.at[turn], sibling)

    def each_peer(turn, act):
        for i in range(chips - 1) if turn != 1 else range(chips - 2, -1, -1):
            act(i + (i >= chip).astype(jnp.int32))

    def gather_start(turn, buffer):
        piece = buffer.at[core, chip]

        def send_one(peer):
            remote(
                piece, piece, chip_send.at[turn], plane_recv.at[shift_of(peer)],
                seat_of(peer, core),
            ).start()

        each_peer(turn, send_one)

    def gather_finish(turn, buffer):
        for step in [0,1,3,2]:
            group = buffer.at[core, pl.ds(0, near if step else near - 1)]
            remote(
                group, group, chip_send.at[turn], plane_recv.at[step], sibling
            ).wait_recv()
            to_sibling(turn, buffer, step).start()
        remote(
            buffer.at[other], buffer.at[other], side_send.at[turn], side_recv.at[turn], sibling
        ).wait_recv()

    def gather_sent(turn, buffer):
        some = buffer.at[0, pl.ds(0, chips - 1)]
        remote(some, some, chip_send.at[turn], plane_recv.at[0], sibling).wait_send()
        remote(
            buffer.at[0], buffer.at[0], side_send.at[turn], side_recv.at[turn], sibling
        ).wait_send()

    loads["core"].wait()
    parts[core, chip] = core_ref[...].astype(jnp.bfloat16)
    def halo_copy(wide, turn, slot):
        dr, dc = NEIGHBOURS[slot]
        inner = slice(1, rows + 1)
        source = {-1: slice(1, 2), 0: inner, 1: slice(rows, rows + 1)}[dr]
        edge = {-1: slice(0, 1), 0: slice(0, cols), 1: slice(cols - 1, cols)}[dc]
        target = {-1: slice(rows + 1, rows + 2), 0: inner, 1: slice(0, 1)}[dr]
        side = 0 if dc == 0 else 1 if n_cols == 2 else 1 + (dc + 1) // 2
        return pltpu.make_async_remote_copy(
            src_ref=wide.at[1, 1 : frames + 1, source, edge],
            dst_ref=wide.at[1 - dc, 1 : frames + 1, target, edge],
            send_sem=halo_send.at[turn, dr + 1, side],
            recv_sem=halo_recv.at[turn, dr + 1, side],
            device_id=(my_row + dr, my_col + dc),
            device_id_type=MESH,
        )

    def there(dr, dc):
        row, col = my_row + dr, my_col + dc
        return (row >= 0) & (row < n_rows) & (col >= 0) & (col < n_cols)

    def halo_each(wide, turn, act, sign):
        for slot, (dr, dc) in enumerate(NEIGHBOURS):
            if (dr != 0 and n_rows == 1) or (dc != 0 and n_cols == 1):
                continue

            @pl.when(there(sign * dr, sign * dc))
            def _():
                act(halo_copy(wide, turn, slot))

    loads["u_in"].wait()
    perm = pair_matrix(rank)
    u_in = dot(perm, uin_ref[...], ((1,), (0,))).astype(jnp.bfloat16)
    pair_ref[...] = dot(uin_ref[...], perm, ((0,), (1,))).astype(jnp.bfloat16)
    loads["x"].wait()
    x = x_ref[...].astype(jnp.float32).reshape(cells, chans).astype(jnp.bfloat16)
    in_proj = dot(x, u_in, ((1,), (1,))).astype(jnp.bfloat16).astype(jnp.float32)
    wide_in[1, 1 : frames + 1, 1 : rows + 1] = in_proj.reshape(frames, rows, cols, rank)
    pl.semaphore_wait(barrier, n - 1)
    halo_each(wide_in, 0, lambda copy: copy.start(), 1)
    gather_start(0, parts)
    halo_each(wide_in, 0, lambda copy: copy.wait_recv(), -1)
    fill_taps(wide_in, taps_in, False)
    gather_finish(0, parts)
    cube_rows(parts, grid_shape, flat, cube)

    mid = dot(taps_in[...], cube[...], ((1,), (0,))).astype(jnp.bfloat16)
    loads["u_out"].wait()
    u_out = uout_ref[...]
    pre = dot(mid, u_out, ((1,), (0,)))
    loads["cot"].wait()
    cot = cot_ref[...].astype(jnp.float32).reshape(cells, chans)
    sig = 1.0 / (1.0 + jnp.exp(-pre))
    slope = (cot * sig * (1.0 + pre * (1.0 - sig))).astype(jnp.bfloat16)
    out_proj = dot(slope, u_out, ((1,), (1,))).astype(jnp.bfloat16)
    wide_out[1, 1 : frames + 1, 1 : rows + 1] = out_proj.astype(jnp.float32).reshape(
        frames, rows, cols, rank
    )
    halo_each(wide_out, 1, lambda copy: copy.start(), 1)

    grad = dot(taps_in[...], out_proj, ((0,), (0,)))
    taps = grad.shape[0] // rank
    half = rank // 2
    grad = grad.reshape(taps, rank, rank)
    grad = jnp.concatenate([grad[:, :half], grad[:, half:]], axis=2)
    flat[...] = grad.reshape(taps * half, 2 * rank)
    part = core_ref.shape[0]
    for owner in range(n):
        on_core, on_chip = seat(owner, n_cols)
        mine[on_core, on_chip] = flat[owner * part : (owner + 1) * part, :].astype(jnp.bfloat16)
    pair_up = remote(mine.at[other], theirs, side_send.at[1], side_recv.at[1], sibling)
    pair_up.start()
    pair_up.wait_recv()
    for k in range(chips):
        send[k] = (mine[core, k].astype(jnp.float32) + theirs[k].astype(jnp.float32)).astype(
            jnp.bfloat16
        )

    def share(peer):
        remote(
            send.at[peer], recv.at[chip], chip_send.at[1], sum_recv.at[0], seat_of(peer, core)
        ).start()

    each_peer(1, share)
    recv[chip] = send[chip]

    halo_each(wide_out, 1, lambda copy: copy.wait_recv(), -1)
    fill_taps(wide_out, taps_out, True)
    total = jnp.zeros((cells, rank), jnp.float32)
    for tap in range(taps):
        span = slice(rank * tap, rank * (tap + 1))
        total = total + dot(taps_out[:, span], cube[span, :], ((1,), (1,)))
    back = dot(total.astype(jnp.bfloat16), u_in, ((1,), (0,)))
    fg_ref[...] = back.reshape(frames, rows, cols, chans).astype(jnp.bfloat16)

    halo_each(wide_in, 0, lambda copy: copy.wait_send(), 1)
    halo_each(wide_out, 1, lambda copy: copy.wait_send(), 1)
    gather_sent(0, parts)
    pair_up.wait_send()
    loads["one"].wait()
    loads["two"].wait()
    some = recv.at[pl.ds(0, chips - 1)]
    shares = remote(some, some, chip_send.at[1], sum_recv.at[0], sibling)
    shares.wait_recv()
    summed = recv[0].astype(jnp.float32)
    for k in range(1, chips):
        summed = summed + recv[k].astype(jnp.float32)
    core_grad = summed / math.sqrt(cells_total)
    one_next = beta_one * one_ref[...] + (1.0 - beta_one) * core_grad
    two_next = beta_two * two_ref[...] + (1.0 - beta_two) * core_grad * core_grad
    core_next = core_ref[...] - learn_rate * (one_next / fix_one) / (
        jnp.sqrt(two_next / fix_two) + epsilon
    )
    parts_next[core, chip] = core_next.astype(jnp.bfloat16)
    gather_start(2, parts_next)
    core_out[...] = core_next
    one_out[...] = one_next
    two_out[...] = two_next
    shares.wait_send()
    gather_finish(2, parts_next)
    cube_rows(parts_next, grid_shape, flat, cube_out)
    gather_sent(2, parts_next)


def build_kernel(
    group, run, cube_ref, uin_ref, uout_ref, fg_from, core_from, one_from, two_from,
    out_hbm, fg_to, core_to, one_to, two_to, out_ref, side_sem, out_sem,
):
    rank = uin_ref.shape[1]
    inner = (fg_from, core_from, one_from, two_from)
    final = (fg_to, core_to, one_to, two_to)
    sides = [
        pltpu.make_async_copy(source, target, side_sem.at[i])
        for i, (source, target) in enumerate(zip(inner, final))
    ]
    u_in = uin_ref[...]
    u_out = uout_ref[...]
    for side in sides:
        side.start()
    copies = []
    for first in range(0, out_ref.shape[0], group):
        cube = cube_ref[rank * first : rank * (first + group), :]
        halfway = dot(cube, u_out, ((1,), (0,))).astype(jnp.bfloat16)
        for tap in range(group):
            span = slice(rank * tap, rank * (tap + 1))
            out_ref[first + tap] = dot(u_in, halfway[span], ((1,), (0,))).astype(jnp.bfloat16)
            if (tap + 1) % run == 0:
                block = pl.ds(first + tap + 1 - run, run)
                copy = pltpu.make_async_copy(
                    out_ref.at[block], out_hbm.at[block], out_sem.at[len(copies)]
                )
                copy.start()
                copies.append(copy)
    for copy in sides + copies:
        copy.wait()


def fused_body(frames_in, cotangent, core, moment_one, moment_two, u_in, u_out):
    frames, rows, cols, chans = frames_in.shape
    rank = u_in.shape[1]
    grid_shape = (lax.axis_size("rows"), lax.axis_size("cols"))
    n = grid_shape[0] * grid_shape[1]
    chips = n // 2
    lanes = 2 * rank
    part = core.shape[0] // lanes
    taps = n * core.shape[0] // (rank * rank)
    cells = frames * rows * cols
    sides_of = 2 if grid_shape[1] == 2 else 3
    f32, bf16 = jnp.float32, jnp.bfloat16
    hbm = pl.BlockSpec(memory_space=pltpu.HBM)
    vmem = pl.BlockSpec(memory_space=pltpu.VMEM)
    block = pltpu.VMEM(frames_in.shape, bf16)
    flat_vmem = pltpu.VMEM((part, lanes), f32)
    factor = pltpu.VMEM((rank, chans), bf16)
    cube_vmem = pltpu.VMEM((taps * rank, rank), bf16)
    flat_shape = jax.ShapeDtypeStruct((part, lanes), f32)
    wide = pltpu.VMEM((3, frames + 2, rows + 2, cols, rank), f32)
    pieces = pltpu.VMEM((2, chips, part, lanes), bf16)
    sums = pltpu.VMEM((chips, part, lanes), bf16)
    in_hbm = functools.partial(pltpu.with_memory_space_constraint, memory_space=pltpu.HBM)
    in_vmem = functools.partial(pltpu.with_memory_space_constraint, memory_space=pltpu.VMEM)
    *sides, cube_next, uin_next, uout_next = pl.pallas_call(
        functools.partial(step_kernel, grid_shape, cells * n),
        out_shape=(
            block,
            flat_vmem,
            flat_vmem,
            flat_vmem,
            cube_vmem,
            pltpu.VMEM((chans, rank), bf16),
            factor,
        ),
        in_specs=[hbm] * 7,
        out_specs=[vmem] * 7,
        scratch_shapes=[
            block,
            block,
            flat_vmem,
            flat_vmem,
            flat_vmem,
            factor,
            wide,
            wide,
            pltpu.VMEM((cells, taps * rank), bf16),
            pltpu.VMEM((cells, taps * rank), bf16),
            pltpu.VMEM((n * part, lanes), f32),
            pltpu.VMEM((taps * rank, rank), bf16),
            pieces,
            pieces,
            pieces,
            sums,
            sums,
            sums,
            pltpu.SemaphoreType.DMA((2, 3, sides_of)),
            pltpu.SemaphoreType.DMA((2, 3, sides_of)),
            pltpu.SemaphoreType.DMA((3,)),
            pltpu.SemaphoreType.DMA((chips // min(4, chips),)),
            pltpu.SemaphoreType.DMA((1,)),
            pltpu.SemaphoreType.DMA((3,)),
            pltpu.SemaphoreType.DMA((3,)),
            pltpu.SemaphoreType.DMA((7,)),
        ],
        compiler_params=pltpu.CompilerParams(
            collective_id=0, has_side_effects=True, vmem_limit_bytes=vmem_limit
        ),
        name="step",
    )(
        in_hbm(frames_in),
        in_hbm(cotangent),
        in_hbm(core.reshape(part, lanes)),
        in_hbm(moment_one.reshape(part, lanes)),
        in_hbm(moment_two.reshape(part, lanes)),
        in_hbm(u_in.T),
        in_hbm(u_out.T),
    )
    group, run = (9,3)
    kernel_next, fg, core_next, one_next, two_next = pl.pallas_call(
        functools.partial(build_kernel, group, run),
        out_shape=(
            jax.ShapeDtypeStruct((taps, chans, chans), bf16),
            jax.ShapeDtypeStruct(frames_in.shape, bf16),
            flat_shape,
            flat_shape,
            flat_shape,
        ),
        in_specs=[vmem] * 7,
        out_specs=[hbm] * 5,
        scratch_shapes=[
            pltpu.VMEM((taps, chans, chans), bf16),
            pltpu.SemaphoreType.DMA((4,)),
            pltpu.SemaphoreType.DMA((taps // run,)),
        ],
        compiler_params=pltpu.CompilerParams(vmem_limit_bytes=vmem_limit),
        name="build",
    )(*(in_vmem(array) for array in (cube_next, uin_next, uout_next, *sides)))
    return (
        fg,
        core_next.reshape(-1),
        one_next.reshape(-1),
        two_next.reshape(-1),
        kernel_next,
    )


def body(frames_in, cotangent, core, moment_one, moment_two, u_in, u_out):
    lanes = 2 * u_in.shape[1]
    aligned = lanes == 128 and core.shape[0] % lanes == 0 and frames_in.shape[2] == 8
    chips = lax.axis_size("rows") * lax.axis_size("cols") // 2
    if aligned and lax.axis_size("rows") % 2 == 0 and chips & (chips - 1) == 0:
        step = fused_body
    else:
        step = plain_body
    return step(frames_in, cotangent, core, moment_one, moment_two, u_in, u_out)


def solution(mesh):
    in_specs = (
        P(None, "rows", "cols", None),
        P(None, "rows", "cols", None),
        P(("rows", "cols")),
        P(("rows", "cols")),
        P(("rows", "cols")),
        P(),
        P(),
    )
    out_specs = (
        P(None, "rows", "cols", None),
        P(("rows", "cols")),
        P(("rows", "cols")),
        P(("rows", "cols")),
        P(),
    )
    return jax.shard_map(body, mesh=mesh, in_specs=in_specs, out_specs=out_specs, check_vma=False)
```
